32 devices in a mesh: dp: 2 (over x), row: 4 (over z), col: 4 (over y, core).
Axes of the slice: x: 2, y: 2, z: 4, core: 2. Of those that a mesh axis runs over, the one named last changes fastest.
Arguments:
- layer_input: bfloat16 [4096, 1024], P(('dp', 'col'), 'row'), may hold values from -40 to 40
- segment_ids: int32 [2, 2048], P('dp'), may hold values from 0 to 7, never falling along the last dimension, each value on 1 to 512 neighbouring positions
- norm1_gain: float32 [1024], P('row'), may hold values from 0.1 to 1.9
- in_weight: bfloat16 [1024, 3, 1024], P('row', None, 'col'), may hold values from -0.1875 to 0.1875
- conv_weight: float32 [3, 1024], P(None, 'col'), may hold values from -3 to 3
- out_weight: bfloat16 [1024, 1024], P('col', 'row'), may hold values from -0.1875 to 0.1875
- norm2_gain: float32 [1024], P('row'), may hold values from 0.1 to 1.9
- gate_up_weight: bfloat16 [1024, 2, 4608], P('row', None, 'col'), may hold values from -0.1875 to 0.1875
- down_weight: bfloat16 [4608, 1024], P('col', 'row'), may hold values from -0.09375 to 0.09375
- cotangent: bfloat16 [4096, 1024], P(('dp', 'col'), 'row'), may hold values from -6 to 6
Outputs:
- block_out: bfloat16 [4096, 1024], P(('dp', 'col'), 'row')
- grad_x: float32 [4096, 1024], P(('dp', 'col'), 'row')
- grad_norm1: float32 [1024], P('row')
- grad_in: float32 [1024, 3, 1024], P('row', None, 'col')
- grad_conv: float32 [3, 1024], P(None, 'col')
- grad_out: float32 [1024, 1024], P('col', 'row')
- grad_norm2: float32 [1024], P('row')
- grad_gate_up: float32 [1024, 2, 4608], P('row', None, 'col')
- grad_down: float32 [4608, 1024], P('col', 'row')
The draws below stay inside these ranges and needn't reach their ends.
Inputs may be any that keep to these rules, and one draw needn't show every extreme that they name: `segment_ids`: within each sequence the ids never fall; each document has 1 to 512 tokens and one has exactly that many.
All inputs are finite; a program needn't handle non-finite values.
Results may differ from the reference program's by a relative error of at most 0.0092.
Values may be sent and summed in bfloat16 or wider, within the bound.
A program may use at most 128 MiB of HBM per device.

```python
import math
import jax
import jax.numpy as jnp
import numpy as np
from jax import lax

D = 1024
FF = 4608
SEGS = 8
SEQ = 2048
TOKENS = 4096
N_DP = 2


def draw_layer_input(key, part):
    key_base, key_rows = jax.random.split(key, 2)
    feature_ramp = jnp.arange(D, dtype=jnp.float32) / (D - 1)
    rows_scale = 0.3 * jnp.exp(jax.random.uniform(key_rows, (TOKENS, 1), jnp.float32, 0.0, math.log(10.0)))
    cols_scale = 0.5 * jnp.exp(feature_ramp * math.log(3.0))
    base_draw = jnp.clip(jax.random.normal(key_base, (TOKENS, D), jnp.float32), -4.0, 4.0)
    return (base_draw * rows_scale * cols_scale).astype(jnp.bfloat16)


def block_scale(stream_key, extent, cuts, smallest, high):
    def one(dim, parts):
        draws = jax.random.uniform(jax.random.fold_in(jax.random.fold_in(stream_key, 6), dim), (parts,), jnp.float32, smallest / len(cuts), high / len(cuts))
        return jnp.repeat(jnp.exp(draws), extent[dim] // parts).reshape((-1,) + (1,) * (len(extent) - dim - 1))

    gain = one(*cuts[0])
    for cut in cuts[1:]:
        gain = gain * one(*cut)
    return gain


def length_profile(count, total, reach, lean):
    weights = [(1 << 20) // math.isqrt(grade ** lean) + 1 for grade in range(2, count + 1)]
    surplus, holding = total - reach - (count - 1), [1] * (count - 1)
    while surplus > 0:
        candidates = [i for i in range(count - 1) if holding[i] < reach]
        pool, left = sum([weights[i] for i in candidates]), surplus
        for i in candidates:
            more = min(reach - holding[i], max(1, left * weights[i] // pool), surplus)
            holding[i] = holding[i] + more
            surplus = surplus - more
    return np.array([reach] + holding)


def uneven(rng, count, total, limit, slope):
    if count == 2:
        one = jax.random.randint(rng, (), max(1, total - limit), min(limit, total - 1) + 1)
        return jnp.stack([one, total - one])
    tallies = jnp.asarray(length_profile(count, total, limit, slope), jnp.int32)
    pairs = (count - 1) // 2
    giver, receiver = tallies[1:1 + 2 * pairs:2], tallies[2:2 + 2 * pairs:2]
    slack = jnp.minimum(giver - 1, limit - receiver)
    passed = jax.random.randint(jax.random.fold_in(rng, 1), (pairs,), 0, 1 << 20) % (slack + 1)
    tallies = tallies.at[1:1 + 2 * pairs:2].set(giver - passed).at[2:2 + 2 * pairs:2].set(receiver + passed)
    return tallies[jax.random.permutation(jax.random.fold_in(rng, 2), count)]


def bell_draw(stream_key, dims, spread, bound, cuts=(), kind=jnp.bfloat16):
    gain = block_scale(stream_key, dims, cuts, -0.22, 0.18) if cuts else 1.0
    entries = jax.random.normal(stream_key, dims, jnp.float32) * spread * gain
    return jnp.minimum(jnp.maximum(entries, -bound), bound).astype(kind)


def setup_inputs(seed: int = 0) -> dict:
    keys = jax.random.split(jax.random.key(seed), 11)
    return {
        "layer_input": draw_layer_input(jax.random.fold_in(keys[10], 71), 0),
        "segment_ids": jax.vmap(lambda own: jnp.searchsorted(jnp.cumsum(uneven(own, SEGS, SEQ, SEQ // 4, 0)), jnp.arange(SEQ), side="right"))(jax.random.split(keys[1], N_DP)).reshape((N_DP, SEQ)).astype(jnp.int32),
        "norm1_gain": jnp.clip(1.0 + 0.18 * jax.random.normal(keys[2], (D,), jnp.float32), 0.1, 1.9),
        "in_weight": bell_draw(keys[3], (D, 3, D), D ** -0.5, 0.1875, ((0, 4), (2, 4))),
        "conv_weight": bell_draw(keys[4], (3, D), 0.6, 3.0, ((1, 4),), jnp.float32),
        "out_weight": bell_draw(keys[5], (D, D), D ** -0.5, 0.1875, ((0, 4), (1, 4))),
        "norm2_gain": jnp.clip(1.0 + 0.18 * jax.random.normal(keys[6], (D,), jnp.float32), 0.1, 1.9),
        "gate_up_weight": bell_draw(keys[7], (D, 2, FF), D ** -0.5, 0.1875, ((0, 4), (2, 4))),
        "down_weight": bell_draw(keys[8], (FF, D), FF ** -0.5, 0.09375, ((0, 4), (1, 4))),
        "cotangent": bell_draw(keys[9], (TOKENS, D), 1.0, 6.0, ((0, 8), (1, 4))),
    }


EPSILON = 1e-05

def conv_masks(seg_row):
    padded = jnp.concatenate([jnp.full((2,), -1, jnp.int32), seg_row.astype(jnp.int32)])
    mask_one = (padded[1:SEQ + 1] == seg_row.astype(jnp.int32)).astype(jnp.float32)[:, None]
    mask_two = (padded[0:SEQ] == seg_row.astype(jnp.int32)).astype(jnp.float32)[:, None]
    return (mask_one, mask_two)

def norm_back(inputs, scales, gains, grads):
    gained = gains * grads
    dots = lax.optimization_barrier(jnp.mean(gained * inputs, axis=1))
    return scales[:, None] * gained - inputs * (scales * scales * scales)[:, None] * dots[:, None]

def reference(layer_input, segment_ids, norm1_gain, in_weight, conv_weight, out_weight, norm2_gain, gate_up_weight, down_weight, cotangent):
    flat_in = in_weight.reshape(D, 3 * D)
    flat_gu = gate_up_weight.reshape(D, 2 * FF)

    def seq_step(carried, items):
        x_rows, seg_row, cot_rows = items
        x_wide = x_rows.astype(jnp.float32)
        scale_one = lax.rsqrt(lax.optimization_barrier(jnp.mean(x_wide * x_wide, axis=1)) + EPSILON)
        x_normed = (x_wide * scale_one[:, None] * norm1_gain).astype(jnp.bfloat16)
        mixed_in = jnp.dot(x_normed, flat_in, preferred_element_type=jnp.float32).reshape(SEQ, 3, D)
        b_gate = mixed_in[:, 0]
        c_gate = mixed_in[:, 1]
        v_part = mixed_in[:, 2]
        gated_in = b_gate * v_part
        mask_one, mask_two = conv_masks(seg_row)
        padded = jnp.concatenate([jnp.zeros((2, D), jnp.float32), gated_in])
        prev_one = padded[1:SEQ + 1]
        prev_two = padded[0:SEQ]
        conv_out = conv_weight[0] * gated_in + conv_weight[1] * mask_one * prev_one + conv_weight[2] * mask_two * prev_two
        mixer_out = (c_gate * conv_out).astype(jnp.bfloat16)
        resid = x_wide + jnp.dot(mixer_out, out_weight, preferred_element_type=jnp.float32)
        scale_two = lax.rsqrt(lax.optimization_barrier(jnp.mean(resid * resid, axis=1)) + EPSILON)
        h_normed = (resid * scale_two[:, None] * norm2_gain).astype(jnp.bfloat16)
        gate_up = jnp.dot(h_normed, flat_gu, preferred_element_type=jnp.float32).reshape(SEQ, 2, FF)
        gate_pre = gate_up[:, 0]
        up_pre = gate_up[:, 1]
        gate_sig = jax.nn.sigmoid(gate_pre)
        hidden = (gate_pre * gate_sig * up_pre).astype(jnp.bfloat16)
        block_out = (resid + jnp.dot(hidden, down_weight, preferred_element_type=jnp.float32)).astype(jnp.bfloat16)
        grad_down = jnp.dot(hidden.T, cot_rows, preferred_element_type=jnp.float32)
        grad_hidden = jnp.dot(cot_rows, down_weight.T, preferred_element_type=jnp.float32)
        grad_gu = jnp.stack([grad_hidden * up_pre * gate_sig * (1.0 + gate_pre * (1.0 - gate_sig)), grad_hidden * gate_pre * gate_sig], axis=1).astype(jnp.bfloat16)
        flat_ggu = grad_gu.reshape(SEQ, 2 * FF)
        grad_gate_up = jnp.dot(h_normed.T, flat_ggu, preferred_element_type=jnp.float32).reshape(D, 2, FF)
        grad_hn = jnp.dot(flat_ggu, flat_gu.T, preferred_element_type=jnp.float32)
        grad_norm2 = lax.optimization_barrier(jnp.sum(grad_hn * resid * scale_two[:, None], axis=0))
        grad_resid = cot_rows.astype(jnp.float32) + norm_back(resid, scale_two, norm2_gain, grad_hn)
        resid_cast = grad_resid.astype(jnp.bfloat16)
        grad_out = jnp.dot(mixer_out.T, resid_cast, preferred_element_type=jnp.float32)
        grad_mixer = jnp.dot(resid_cast, out_weight.T, preferred_element_type=jnp.float32)
        grad_conv_out = grad_mixer * c_gate
        grad_c = grad_mixer * conv_out
        grad_conv = jnp.stack([lax.optimization_barrier(jnp.sum(grad_conv_out * gated_in, axis=0)), lax.optimization_barrier(jnp.sum(grad_conv_out * mask_one * prev_one, axis=0)), lax.optimization_barrier(jnp.sum(grad_conv_out * mask_two * prev_two, axis=0))])
        later_one = conv_weight[1] * mask_one * grad_conv_out
        later_two = conv_weight[2] * mask_two * grad_conv_out
        grad_gated = conv_weight[0] * grad_conv_out + jnp.concatenate([later_one[1:], jnp.zeros((1, D), jnp.float32)]) + jnp.concatenate([later_two[2:], jnp.zeros((2, D), jnp.float32)])
        grad_mixed = jnp.stack([grad_gated * v_part, grad_c, grad_gated * b_gate], axis=1).astype(jnp.bfloat16)
        flat_gm = grad_mixed.reshape(SEQ, 3 * D)
        grad_in = jnp.dot(x_normed.T, flat_gm, preferred_element_type=jnp.float32).reshape(D, 3, D)
        grad_xn = jnp.dot(flat_gm, flat_in.T, preferred_element_type=jnp.float32)
        grad_norm1 = lax.optimization_barrier(jnp.sum(grad_xn * x_wide * scale_one[:, None], axis=0))
        grad_x = grad_resid + norm_back(x_wide, scale_one, norm1_gain, grad_xn)
        sums = (grad_norm1, grad_in, grad_conv, grad_out, grad_norm2, grad_gate_up, grad_down)
        carried = jax.tree.map(lambda left, right: left + right, carried, sums)
        return (carried, (block_out, grad_x))
    start = (jnp.zeros((D,), jnp.float32), jnp.zeros((D, 3, D), jnp.float32), jnp.zeros((3, D), jnp.float32), jnp.zeros((D, D), jnp.float32), jnp.zeros((D,), jnp.float32), jnp.zeros((D, 2, FF), jnp.float32), jnp.zeros((FF, D), jnp.float32))
    sums, (outputs, grads_x) = lax.scan(seq_step, start, (layer_input.reshape(N_DP, SEQ, D), segment_ids, cotangent.reshape(N_DP, SEQ, D)))
    return (outputs.reshape(TOKENS, D), grads_x.reshape(TOKENS, D), sums[0], sums[1], sums[2], sums[3], sums[4], sums[5], sums[6])
```

```python
import jax
import jax.numpy as jnp
from jax import lax
from jax.sharding import PartitionSpec as P

EPSILON = 1e-05
BF = jnp.bfloat16
F32 = jnp.float32


def swapped(block, axis, distance):
    size = lax.axis_size(axis)
    return lax.ppermute(block, axis, [(i, i ^ distance) for i in range(size)])


def rotated(block, axis, distance):
    size = lax.axis_size(axis)
    return lax.ppermute(block, axis, [(i, (i + distance) % size) for i in range(size)])


def pick(blocks, index):
    return lax.dynamic_index_in_dim(blocks, index, 0, keepdims=False)


def to_tokens(local, place):
    size = lax.axis_size("row")
    quarters = local.reshape(size, local.shape[0] // size, local.shape[1])
    parts = [pick(quarters, place)]
    for k in range(1, size):
        parts.append(swapped(pick(quarters, place ^ k), "row", k))
    stacked = jnp.stack(parts)
    return jnp.concatenate([pick(stacked, place ^ r) for r in range(size)], axis=1)


def to_features(local, place):
    size = lax.axis_size("row")
    tokens, width = local.shape
    feats = width // size
    blocks = local.reshape(tokens, size, feats).transpose(1, 0, 2)
    parts = [pick(blocks, place)]
    for k in range(1, size):
        parts.append(swapped(pick(blocks, place ^ k), "row", k))
    stacked = jnp.stack(parts)
    return jnp.concatenate([pick(stacked, place ^ r) for r in range(size)], axis=0)


def spread_cols(own):
    size = lax.axis_size("col")
    return jnp.concatenate([own] + [swapped(own, "col", k) for k in range(1, size)], axis=0)


def summed_cols(partial):
    size = lax.axis_size("col")
    blocks = partial.reshape((size, partial.shape[0] // size) + partial.shape[1:])
    total = blocks[0]
    for k in range(1, size):
        total = total + swapped(blocks[k].astype(BF), "col", k).astype(F32)
    return total


def summed_rows(blocks):
    return lax.psum_scatter(blocks.astype(BF), "row", scatter_dimension=0, tiled=True)


def summed_dp(block):
    if lax.axis_size("dp") != 2:
        return lax.psum(block.astype(F32), "dp")
    return block.astype(F32) + swapped(block, "dp", 1).astype(F32)


def summed_everywhere(block):
    for axis in ("col", "row", "dp"):
        distance = 1
        while distance < lax.axis_size(axis):
            block = block + swapped(block, axis, distance)
            distance *= 2
    return block


def norm_scale(inputs):
    return lax.rsqrt(jnp.mean(inputs * inputs, axis=1, keepdims=True) + EPSILON)


def norm_back(inputs, scales, gains, grads):
    gained = gains * grads
    dots = jnp.mean(gained * inputs, axis=1, keepdims=True)
    return scales * gained - inputs * (scales * scales * scales) * dots


def mm(form, a, b):
    return jnp.einsum(form, a, b, preferred_element_type=F32)


def on_device(
    layer_input,
    segment_ids,
    norm1_gain,
    in_weight,
    conv_weight,
    out_weight,
    norm2_gain,
    gate_up_weight,
    down_weight,
    cotangent,
):
    rows = lax.axis_size("row")
    cols = lax.axis_size("col")
    row = lax.axis_index("row")
    col = lax.axis_index("col")
    seq_len = segment_ids.shape[1]
    piece = seq_len // (rows * cols)
    tokens = cols * piece
    row_feats = layer_input.shape[1]
    width = rows * row_feats
    col_feats = conv_weight.shape[1]

    in_all = lax.all_gather(in_weight, "row", axis=0, tiled=True)
    out_all = lax.all_gather(out_weight, "row", axis=0)
    gu_all = lax.all_gather(gate_up_weight, "row", axis=0, tiled=True)
    down_all = lax.all_gather(down_weight, "row", axis=0)
    gains = lax.all_gather(jnp.stack([norm1_gain, norm2_gain]), "row", axis=1, tiled=True)
    gain_one, gain_two = gains[0], gains[1]

    x_own = to_tokens(layer_input, row).astype(F32)
    cot_own = to_tokens(cotangent, row)
    cot_all = spread_cols(cot_own)

    ids = segment_ids[0]
    padded = jnp.concatenate([jnp.full((2,), -1, jnp.int32), ids])
    masks = jnp.stack([padded[1 : seq_len + 1] == ids, padded[0:seq_len] == ids])
    masks = masks.astype(F32).reshape(2, cols, rows, piece)
    masks = lax.dynamic_index_in_dim(masks, row, 2, keepdims=False)
    masks = jnp.stack(
        [lax.dynamic_index_in_dim(masks, col ^ j, 1, keepdims=False) for j in range(cols)], axis=1
    )
    mask_one = masks[0][:, :, None]
    mask_two = masks[1][:, :, None]

    scale_one = norm_scale(x_own)
    x_normed = (x_own * scale_one * gain_one).astype(BF)
    xn_all = spread_cols(x_normed)
    mixed = mm("td,dkf->tkf", xn_all, in_all).reshape(cols, piece, 3, col_feats)
    b_gate = mixed[:, :, 0]
    c_gate = mixed[:, :, 1]
    v_part = mixed[:, :, 2]
    gated_in = b_gate * v_part
    tails = rotated(gated_in[:, piece - 2 :], "row", 1)
    before = [
        pick(tails, jnp.where(row > 0, j, jnp.maximum((col ^ j) - 1, 0) ^ col)) for j in range(cols)
    ]
    extended = jnp.concatenate([jnp.stack(before), gated_in], axis=1)
    prev_one = extended[:, 1 : piece + 1] * mask_one
    prev_two = extended[:, 0:piece] * mask_two
    conv_out = conv_weight[0] * gated_in + conv_weight[1] * prev_one + conv_weight[2] * prev_two
    mixer_out = (c_gate * conv_out).astype(BF).reshape(tokens, col_feats)
    resid = x_own + summed_cols(mm("tf,rfd->trd", mixer_out, out_all).reshape(tokens, width))
    scale_two = norm_scale(resid)
    h_normed = (resid * scale_two * gain_two).astype(BF)
    hn_all = spread_cols(h_normed)

    gate_up = mm("td,dkf->tkf", hn_all, gu_all)
    gate_pre = gate_up[:, 0]
    up_pre = gate_up[:, 1]
    sig = jax.nn.sigmoid(gate_pre)
    hidden = (gate_pre * sig * up_pre).astype(BF)
    cot_split = cot_all.reshape(tokens, rows, row_feats)
    grad_down = summed_rows(mm("tf,trd->rfd", hidden, cot_split))[0]
    grad_hidden = mm("trd,rfd->tf", cot_split, down_all)
    grad_gu = jnp.stack(
        [
            grad_hidden * up_pre * sig * (1.0 + gate_pre * (1.0 - sig)),
            grad_hidden * gate_pre * sig,
        ],
        axis=1,
    ).astype(BF)
    grad_hn = summed_cols(mm("tkf,dkf->td", grad_gu, gu_all))
    grad_gate_up = summed_rows(mm("td,tkf->dkf", hn_all, grad_gu))
    block_own = resid + summed_cols(mm("tf,rfd->trd", hidden, down_all).reshape(tokens, width))
    block_out = to_features(block_own.astype(BF), row)

    norm2_part = jnp.sum(grad_hn * resid * scale_two, axis=0)
    grad_resid = cot_own.astype(F32) + norm_back(resid, scale_two, gain_two, grad_hn)
    rcast_all = spread_cols(grad_resid.astype(BF))
    rcast_split = rcast_all.reshape(tokens, rows, row_feats)
    grad_mixer = mm("trd,rfd->tf", rcast_split, out_all).reshape(cols, piece, col_feats)
    grad_out = summed_rows(mm("tf,trd->rfd", mixer_out, rcast_split))[0]

    grad_conv_out = grad_mixer * c_gate
    conv_part = jnp.stack(
        [
            jnp.sum(grad_conv_out * gated_in, axis=(0, 1)),
            jnp.sum(grad_conv_out * prev_one, axis=(0, 1)),
            jnp.sum(grad_conv_out * prev_two, axis=(0, 1)),
        ]
    )
    later_one = conv_weight[1] * mask_one * grad_conv_out
    later_two = conv_weight[2] * mask_two * grad_conv_out
    heads = rotated(jnp.concatenate([later_one[:, 0:1], later_two[:, 0:2]], axis=1), "row", -1)
    after = jnp.stack(
        [
            pick(heads, jnp.where(row < rows - 1, j, jnp.minimum((col ^ j) + 1, cols - 1) ^ col))
            * jnp.where((row == rows - 1) & ((col ^ j) == cols - 1), 0.0, 1.0)
            for j in range(cols)
        ]
    )
    grad_gated = (
        conv_weight[0] * grad_conv_out
        + jnp.concatenate([later_one[:, 1:], after[:, 0:1]], axis=1)
        + jnp.concatenate([later_two[:, 2:], after[:, 1:3]], axis=1)
    )
    grad_mixed = (
        jnp.stack([grad_gated * v_part, grad_mixer * conv_out, grad_gated * b_gate], axis=2)
        .astype(BF)
        .reshape(tokens, 3, col_feats)
    )
    grad_in = summed_rows(mm("td,tkf->dkf", xn_all, grad_mixed))
    grad_xn = summed_cols(mm("tkf,dkf->td", grad_mixed, in_all))
    norm1_part = jnp.sum(grad_xn * x_own * scale_one, axis=0)
    grad_own = grad_resid + norm_back(x_own, scale_one, gain_one, grad_xn)
    grad_x = to_features(grad_own.astype(BF), row).astype(F32)

    conv_padded = lax.dynamic_update_slice_in_dim(
        jnp.zeros((3, cols * col_feats), F32), conv_part, col * col_feats, 1
    )
    small = summed_everywhere(
        jnp.concatenate([conv_padded, norm1_part[None], norm2_part[None]], axis=0)
    )
    conv_own = lax.dynamic_slice_in_dim(small[0:3], col * col_feats, col_feats, 1)
    gain_own = lax.dynamic_slice_in_dim(small[3:5], row * row_feats, row_feats, 1)
    return (
        block_out,
        grad_x,
        gain_own[0],
        summed_dp(grad_in),
        conv_own,
        summed_dp(grad_out),
        gain_own[1],
        summed_dp(grad_gate_up),
        summed_dp(grad_down),
    )


def solution(mesh):
    return jax.shard_map(
        on_device,
        mesh=mesh,
        in_specs=(
            P(("dp", "col"), "row"),
            P("dp", None),
            P("row"),
            P("row", None, "col"),
            P(None, "col"),
            P("col", "row"),
            P("row"),
            P("row", None, "col"),
            P("col", "row"),
            P(("dp", "col"), "row"),
        ),
        out_specs=(
            P(("dp", "col"), "row"),
            P(("dp", "col"), "row"),
            P("row"),
            P("row", None, "col"),
            P(None, "col"),
            P("col", "row"),
            P("row"),
            P("row", None, "col"),
            P("col", "row"),
        ),
        check_vma=False,
    )
```

```python
import jax
import jax.numpy as jnp
from jax import lax
from jax.sharding import PartitionSpec as P

EPSILON = 1e-05
BF = jnp.bfloat16
F32 = jnp.float32


def swapped(block, axis, distance):
    size = lax.axis_size(axis)
    return lax.ppermute(block, axis, [(i, i ^ distance) for i in range(size)])


def rotated(block, axis, distance):
    size = lax.axis_size(axis)
    return lax.ppermute(block, axis, [(i, (i + distance) % size) for i in range(size)])


def pick(blocks, index):
    return lax.dynamic_index_in_dim(blocks, index, 0, keepdims=False)


def to_tokens(local, place):
    size = lax.axis_size("row")
    quarters = local.reshape(size, local.shape[0] // size, local.shape[1])
    parts = [pick(quarters, place)]
    for k in range(1, size):
        parts.append(swapped(pick(quarters, place ^ k), "row", k))
    stacked = jnp.stack(parts)
    return jnp.concatenate([pick(stacked, place ^ r) for r in range(size)], axis=1)


def to_features(local, place):
    size = lax.axis_size("row")
    tokens, width = local.shape
    feats = width // size
    blocks = local.reshape(tokens, size, feats).transpose(1, 0, 2)
    parts = [pick(blocks, place)]
    for k in range(1, size):
        parts.append(swapped(pick(blocks, place ^ k), "row", k))
    stacked = jnp.stack(parts)
    return jnp.concatenate([pick(stacked, place ^ r) for r in range(size)], axis=0)


def spread_gains(own, place):
    size = lax.axis_size("row")
    stacked = jnp.stack([own] + [swapped(own, "row", k) for k in range(1, size)])
    return jnp.concatenate([pick(stacked, place ^ r) for r in range(size)], axis=1)


def spread_cols(own):
    size = lax.axis_size("col")
    return jnp.concatenate([own] + [swapped(own, "col", k) for k in range(1, size)], axis=0)


def summed_cols(partial):
    size = lax.axis_size("col")
    blocks = partial.reshape((size, partial.shape[0] // size) + partial.shape[1:])
    total = blocks[0]
    for k in range(1, size):
        total = total + swapped(blocks[k].astype(BF), "col", k).astype(F32)
    return total


def summed_rows(blocks):
    return lax.psum_scatter(blocks.astype(BF), "row", scatter_dimension=0, tiled=True)


def summed_dp(block):
    if lax.axis_size("dp") != 2:
        return lax.psum(block.astype(F32), "dp")
    return block.astype(F32) + swapped(block, "dp", 1).astype(F32)


def summed_everywhere(block):
    for axis in ("col", "row", "dp"):
        distance = 1
        while distance < lax.axis_size(axis):
            block = block + swapped(block, axis, distance)
            distance *= 2
    return block


def norm_scale(inputs):
    return lax.rsqrt(jnp.mean(inputs * inputs, axis=1, keepdims=True) + EPSILON)


def norm_back(inputs, scales, gains, grads):
    gained = gains * grads
    dots = jnp.mean(gained * inputs, axis=1, keepdims=True)
    return scales * gained - inputs * (scales * scales * scales) * dots


def mm(form, a, b):
    return jnp.einsum(form, a, b, preferred_element_type=F32)


def on_device(
    layer_input,
    segment_ids,
    norm1_gain,
    in_weight,
    conv_weight,
    out_weight,
    norm2_gain,
    gate_up_weight,
    down_weight,
    cotangent,
):
    rows = lax.axis_size("row")
    cols = lax.axis_size("col")
    row = lax.axis_index("row")
    col = lax.axis_index("col")
    seq_len = segment_ids.shape[1]
    piece = seq_len // (rows * cols)
    tokens = cols * piece
    row_feats = layer_input.shape[1]
    width = rows * row_feats
    col_feats = conv_weight.shape[1]

    mixer_weights = jnp.concatenate([in_weight, out_weight.T[:, None]], axis=1)
    mixer_weights = lax.all_gather(mixer_weights, "row", axis=0, tiled=True)
    in_all = mixer_weights[:, 0:3]
    out_all = mixer_weights[:, 3]
    gu_all = lax.all_gather(gate_up_weight, "row", axis=0, tiled=True)
    down_all = lax.all_gather(down_weight, "row", axis=0)
    gains = spread_gains(jnp.stack([norm1_gain, norm2_gain]), row)
    gain_one, gain_two = gains[0], gains[1]

    x_own = to_tokens(layer_input, row).astype(F32)
    cot_own = to_tokens(cotangent, row)
    cot_all = spread_cols(cot_own)

    ids = segment_ids[0]
    padded = jnp.concatenate([jnp.full((2,), -1, jnp.int32), ids])
    masks = jnp.stack([padded[1 : seq_len + 1] == ids, padded[0:seq_len] == ids])
    masks = masks.astype(F32).reshape(2, cols, rows, piece)
    masks = lax.dynamic_index_in_dim(masks, row, 2, keepdims=False)
    masks = jnp.stack(
        [lax.dynamic_index_in_dim(masks, col ^ j, 1, keepdims=False) for j in range(cols)], axis=1
    )
    mask_one = masks[0][:, :, None]
    mask_two = masks[1][:, :, None]

    scale_one = norm_scale(x_own)
    x_normed = (x_own * scale_one * gain_one).astype(BF)
    xn_all = spread_cols(x_normed)
    mixed = mm("td,dkf->tkf", xn_all, in_all).reshape(cols, piece, 3, col_feats)
    b_gate = mixed[:, :, 0]
    c_gate = mixed[:, :, 1]
    v_part = mixed[:, :, 2]
    gated_in = b_gate * v_part
    tails = rotated(gated_in[:, piece - 2 :], "row", 1)
    before = [
        pick(tails, jnp.where(row > 0, j, jnp.maximum((col ^ j) - 1, 0) ^ col)) for j in range(cols)
    ]
    extended = jnp.concatenate([jnp.stack(before), gated_in], axis=1)
    prev_one = extended[:, 1 : piece + 1] * mask_one
    prev_two = extended[:, 0:piece] * mask_two
    conv_out = conv_weight[0] * gated_in + conv_weight[1] * prev_one + conv_weight[2] * prev_two
    mixer_out = (c_gate * conv_out).astype(BF).reshape(tokens, col_feats)
    resid = x_own + summed_cols(mm("tf,df->td", mixer_out, out_all))
    scale_two = norm_scale(resid)
    h_normed = (resid * scale_two * gain_two).astype(BF)
    hn_all = spread_cols(h_normed)

    gate_up = mm("td,dkf->tkf", hn_all, gu_all)
    gate_pre = gate_up[:, 0]
    up_pre = gate_up[:, 1]
    sig = jax.nn.sigmoid(gate_pre)
    hidden = (gate_pre * sig * up_pre).astype(BF)
    cot_split = cot_all.reshape(tokens, rows, row_feats)
    down_part = mm("tf,trd->rfd", hidden, cot_split).astype(BF)
    down_part, cot_later = lax.optimization_barrier((down_part, cot_split))
    grad_down = summed_rows(down_part)[0]
    grad_hidden = mm("trd,rfd->tf", cot_later, down_all)
    grad_gu = jnp.stack(
        [
            grad_hidden * up_pre * sig * (1.0 + gate_pre * (1.0 - sig)),
            grad_hidden * gate_pre * sig,
        ],
        axis=1,
    ).astype(BF)
    gate_up_part = mm("td,tkf->dkf", hn_all, grad_gu).astype(BF)
    gate_up_part, grad_gu = lax.optimization_barrier((gate_up_part, grad_gu))
    gate_up_part, grad_down = lax.optimization_barrier((gate_up_part, grad_down))
    grad_gate_up = summed_rows(gate_up_part)
    grad_hn = summed_cols(mm("tkf,dkf->td", grad_gu, gu_all))
    block_own = resid + summed_cols(mm("tf,rfd->trd", hidden, down_all).reshape(tokens, width))
    block_out = to_features(block_own.astype(BF), row)

    norm2_part = jnp.sum(grad_hn * resid * scale_two, axis=0)
    grad_resid = cot_own.astype(F32) + norm_back(resid, scale_two, gain_two, grad_hn)
    rcast_all = spread_cols(grad_resid.astype(BF))
    grad_mixer = mm("td,df->tf", rcast_all, out_all).reshape(cols, piece, col_feats)
    out_part = mm("td,tf->df", rcast_all, mixer_out).astype(BF)

    grad_conv_out = grad_mixer * c_gate
    conv_part = jnp.stack(
        [
            jnp.sum(grad_conv_out * gated_in, axis=(0, 1)),
            jnp.sum(grad_conv_out * prev_one, axis=(0, 1)),
            jnp.sum(grad_conv_out * prev_two, axis=(0, 1)),
        ]
    )
    later_one = conv_weight[1] * mask_one * grad_conv_out
    later_two = conv_weight[2] * mask_two * grad_conv_out
    heads = rotated(jnp.concatenate([later_one[:, 0:1], later_two[:, 0:2]], axis=1), "row", -1)
    after = jnp.stack(
        [
            pick(heads, jnp.where(row < rows - 1, j, jnp.minimum((col ^ j) + 1, cols - 1) ^ col))
            * jnp.where((row == rows - 1) & ((col ^ j) == cols - 1), 0.0, 1.0)
            for j in range(cols)
        ]
    )
    grad_gated = (
        conv_weight[0] * grad_conv_out
        + jnp.concatenate([later_one[:, 1:], after[:, 0:1]], axis=1)
        + jnp.concatenate([later_two[:, 2:], after[:, 1:3]], axis=1)
    )
    grad_mixed = (
        jnp.stack([grad_gated * v_part, grad_mixer * conv_out, grad_gated * b_gate], axis=2)
        .astype(BF)
        .reshape(tokens, 3, col_feats)
    )
    in_part = mm("td,tkf->dkf", xn_all, grad_mixed).astype(BF)
    mixer_part = jnp.concatenate([in_part, out_part[:, None]], axis=1)
    mixer_part, grad_mixed = lax.optimization_barrier((mixer_part, grad_mixed))
    mixer_part, grad_gate_up = lax.optimization_barrier((mixer_part, grad_gate_up))
    grad_mixer_weights = summed_dp(summed_rows(mixer_part))
    grad_xn = summed_cols(mm("tkf,dkf->td", grad_mixed, in_all))
    norm1_part = jnp.sum(grad_xn * x_own * scale_one, axis=0)
    grad_own = grad_resid + norm_back(x_own, scale_one, gain_one, grad_xn)
    grad_x = to_features(grad_own.astype(BF), row).astype(F32)

    conv_padded = lax.dynamic_update_slice_in_dim(
        jnp.zeros((3, cols * col_feats), F32), conv_part, col * col_feats, 1
    )
    small = summed_everywhere(
        jnp.concatenate([conv_padded, norm1_part[None], norm2_part[None]], axis=0)
    )
    conv_own = lax.dynamic_slice_in_dim(small[0:3], col * col_feats, col_feats, 1)
    gain_own = lax.dynamic_slice_in_dim(small[3:5], row * row_feats, row_feats, 1)
    return (
        block_out,
        grad_x,
        gain_own[0],
        grad_mixer_weights[:, 0:3],
        conv_own,
        grad_mixer_weights[:, 3].T,
        gain_own[1],
        summed_dp(grad_gate_up),
        summed_dp(grad_down),
    )


def solution(mesh):
    return jax.shard_map(
        on_device,
        mesh=mesh,
        in_specs=(
            P(("dp", "col"), "row"),
            P("dp", None),
            P("row"),
            P("row", None, "col"),
            P(None, "col"),
            P("col", "row"),
            P("row"),
            P("row", None, "col"),
            P("col", "row"),
            P(("dp", "col"), "row"),
        ),
        out_specs=(
            P(("dp", "col"), "row"),
            P(("dp", "col"), "row"),
            P("row"),
            P("row", None, "col"),
            P(None, "col"),
            P("col", "row"),
            P("row"),
            P("row", None, "col"),
            P("col", "row"),
        ),
        check_vma=False,
    )
```
